256 devices in a mesh: row: 32 (over z_lo, x, core), col: 8 (over z_hi, y).
Axes of the slice: x: 4, y: 4, z: 8 (z_hi: 2, z_lo: 4; z = z_hi * 4 + z_lo), core: 2. Of those that a mesh axis runs over, the one named last changes fastest.
Arguments:
- ancestors: bfloat16 [128, 128, 256, 256], P('row', 'col'), may hold values from -6 to 6
- panel_one: bfloat16 [2, 128, 256, 256], P(None, 'row'), may hold values from -0.0625 to 0.0625
- present_one: int32 [2, 128], replicated, may hold values from 0 to 1, as said below
- dinv_one: bfloat16 [2, 256, 256], replicated, may hold values from -6 to 6
- panel_two: bfloat16 [2, 128, 256, 256], P(None, 'row'), may hold values from -0.0625 to 0.0625
- present_two: int32 [2, 128], replicated, may hold values from 0 to 1, as said below
- dinv_two: bfloat16 [2, 256, 256], replicated, may hold values from -6 to 6
Outputs:
- update_one: float32 [256, 256, 256], P(('row', 'col'))
- diag_one: float32 [2, 256, 256], replicated
- update_two: float32 [256, 256, 256], P(('row', 'col'))
- diag_two: float32 [2, 256, 256], replicated
The draws below stay inside these ranges and needn't reach their ends.
Inputs may be any that keep to these rules, and one draw needn't show every extreme that they name: `present_one`: each supernode's row has 16 to 64 ones, block row 0 among them; the first supernode of each level has exactly 64. `present_two`: each supernode's row has 16 to 64 ones, block row 0 among them; the first supernode of each level has exactly 64.
All inputs are finite; a program needn't handle non-finite values.
Results may differ from the reference program's by a relative error of at most 0.0003.
Values may be sent and summed in bfloat16 or wider, within the bound.
No kernel may reach another device: no remote copies, remote signals or barrier semaphores. Data moves between devices by JAX's collectives and lax.ppermute only.
A program may use at most 128 MiB of HBM per device.

```python
import jax
import jax.numpy as jnp
from jax import lax

B = 256
S = 2
LMIN = 16
LMAX = 64
NA = 128


def pattern_mask(key):
    key_one, key_two = jax.random.split(key)
    noise_span = 131072 // NA
    noise_part = jax.random.randint(key_one, (S, NA), 0, noise_span)
    col_ids = jnp.arange(NA, dtype=jnp.int32)
    scores = noise_part * NA + col_ids[None, :]
    scores = jnp.where(col_ids[None, :] == 0, noise_span * NA + NA, scores)
    ranking = jnp.argsort(-scores, axis=1)
    places = jnp.argsort(ranking, axis=1)
    lengths = jax.random.randint(key_two, (S,), LMIN, LMAX + 1)
    lengths = lengths.at[0].set(LMAX)
    return (places < lengths[:, None]).astype(jnp.int32)


def draw_present_one(key, part):
    return pattern_mask(jax.random.fold_in(key, 11))


def draw_present_two(key, part):
    return pattern_mask(jax.random.fold_in(key, 23))


def block_levels(rng, dims, cuts, least, top_value):
    level, own = 1.0, jax.random.fold_in(rng, 6)
    for axis_at, shards_of in cuts:
        heights = jnp.exp(jax.random.uniform(jax.random.fold_in(own, axis_at), (shards_of,), jnp.float32, least / len(cuts), top_value / len(cuts)))
        level = level * jnp.repeat(heights, dims[axis_at] // shards_of).reshape([-1 if axis == axis_at else 1 for axis in range(len(dims))])
    return level


def bell_draw(own_key, dims, spread, most, cuts=(), held_as=jnp.bfloat16):
    level = block_levels(own_key, dims, cuts, -0.22, 0.18) if cuts else 1.0
    drawn = jax.random.normal(own_key, dims, jnp.float32) * spread * level
    return jnp.minimum(jnp.maximum(drawn, -most), most).astype(held_as)


def setup_inputs(seed: int = 0) -> dict:
    streams_of = jax.random.split(jax.random.key(seed), 8)
    return {
        "ancestors": bell_draw(streams_of[0], (NA, NA, B, B), 1.0, 6.0, ((0, 32), (1, 8))),
        "panel_one": bell_draw(streams_of[1], (S, NA, B, B), (32 * B) ** -0.5, 0.0625, ((1, 32),)),
        "present_one": draw_present_one(jax.random.fold_in(streams_of[7], 71), 0),
        "dinv_one": bell_draw(streams_of[3], (S, B, B), 1.0, 6.0),
        "panel_two": bell_draw(streams_of[4], (S, NA, B, B), (32 * B) ** -0.5, 0.0625, ((1, 32),)),
        "present_two": draw_present_two(jax.random.fold_in(streams_of[7], 71), 0),
        "dinv_two": bell_draw(streams_of[6], (S, B, B), 1.0, 6.0),
    }


def level_reference(ancestors, panel_part, present, inv_diag):
    def one_supernode(level_item):
        lpanel, mask_row, dblock = level_item
        ranking = jnp.argsort(-mask_row, stable=True).astype(jnp.int32)
        chosen = ranking[:LMAX]
        live_rows = jnp.take(mask_row, chosen).astype(jnp.float32)
        chosen_panel = jnp.take(lpanel, chosen, axis=0).astype(jnp.float32) * live_rows[:, None, None]
        right_side = chosen_panel.reshape(LMAX * B, B)

        def row_block(row_index):
            anc_row = jnp.take(jnp.take(ancestors, row_index, axis=0), chosen, axis=0).astype(jnp.float32)
            wide_row = jnp.transpose(anc_row, (1, 0, 2)).reshape(B, LMAX * B)
            return jnp.dot(wide_row, right_side, preferred_element_type=jnp.float32)

        row_products = lax.map(row_block, chosen)
        blocks = -row_products * live_rows[:, None, None]
        full_column = jnp.zeros((NA, B, B), jnp.float32).at[chosen].set(blocks)
        diag_block = dblock.astype(jnp.float32) - jnp.einsum("iba,ibc->ac", chosen_panel, blocks, precision=lax.Precision.HIGHEST)
        return full_column, diag_block

    full_columns, diag_blocks = lax.map(one_supernode, (panel_part, present, inv_diag))
    update = jnp.transpose(full_columns, (1, 0, 2, 3)).reshape(NA * S, B, B)
    return update, diag_blocks


def reference(ancestors, panel_one, present_one, dinv_one, panel_two, present_two, dinv_two):
    update_one, diag_one = level_reference(ancestors, panel_one, present_one, dinv_one)
    update_two, diag_two = level_reference(ancestors, panel_two, present_two, dinv_two)
    return (update_one, diag_one, update_two, diag_two)
```

```python
import functools

import jax
import jax.numpy as jnp
from jax import lax
from jax.experimental import pallas as pl
from jax.experimental.pallas import tpu as pltpu
from jax.sharding import PartitionSpec as P

F32 = jnp.float32
BF16 = jnp.bfloat16
SEND = jnp.float16
AXES = ("row", "col")


def split_id(dev):
    row, col = dev // 8, dev % 8
    return row // 8, (row // 2) % 4, row % 2, col // 4, col % 4


def join_id(zl, x, core, zh, y):
    return ((zl * 4 + x) * 2 + core) * 8 + zh * 4 + y


def send(value, where):
    pairs = [(dev, join_id(*where(*split_id(dev)))) for dev in range(256)]
    return lax.ppermute(value, AXES, pairs)


def to_core(value):
    return send(value, lambda zl, x, core, zh, y: (zl, x, core ^ 1, zh, y))


def to_x(value, k):
    return send(value, lambda zl, x, core, zh, y: (zl, x ^ k, core, zh, y))


def to_zl(value, k):
    return send(value, lambda zl, x, core, zh, y: (zl ^ k, x, core, zh, y))


def to_y(value, k):
    return send(value, lambda zl, x, core, zh, y: (zl, x, core, zh, y ^ k))


def to_zh(value):
    return send(value, lambda zl, x, core, zh, y: (zl, x, core, zh ^ 1, y))


def to_plane(value):
    return send(
        value,
        lambda zl, x, core, zh, y: (y, 2 * (x % 2) + zh, core, zl // 2, 2 * (zl % 2) + x // 2),
    )


def product_kernel(scal, a_ref, p0, p1, p2, p3, d_ref, out_ref, diag_ref):
    step = pl.program_id(0)
    pieces = (p0, p1, p2, p3)
    low = scal[24] & 1

    @pl.when(step == 0)
    def _():
        diag_ref[...] = jnp.zeros_like(diag_ref)

    for k in range(2):
        acc = jnp.zeros((256, 256), F32)
        for pos in range(16):
            block = a_ref[0, scal[pos]]
            acc += jnp.dot(block, pieces[pos // 4][pos % 4, k], preferred_element_type=F32)
        term = acc * (-scal[16 + 2 * step + k]).astype(F32)
        out_ref[k ^ low, 0] = term
        high = term.astype(BF16)
        rest = (term - high.astype(F32)).astype(BF16)
        left = d_ref[k, 0]
        dims = (((0,), (0,)), ((), ()))
        diag_ref[k] += lax.dot_general(left, high, dims, preferred_element_type=F32)
        diag_ref[k] += lax.dot_general(left, rest, dims, preferred_element_type=F32)


def products(scal, blocks, pieces, left):
    whole = lambda i, s: (0, 0, 0, 0)
    return pl.pallas_call(
        product_kernel,
        grid_spec=pltpu.PrefetchScalarGridSpec(
            num_scalar_prefetch=1,
            grid=(4,),
            in_specs=[
                pl.BlockSpec((1, 16, 256, 256), lambda i, s: (i, 0, 0, 0)),
                pl.BlockSpec((4, 2, 256, 256), whole),
                pl.BlockSpec((4, 2, 256, 256), whole),
                pl.BlockSpec((4, 2, 256, 256), whole),
                pl.BlockSpec((4, 2, 256, 256), whole),
                pl.BlockSpec((2, 1, 256, 256), lambda i, s: (0, i, 0, 0)),
            ],
            out_specs=[
                pl.BlockSpec(
                    (2, 1, 256, 256),
                    lambda i, s: ((i % 2) ^ (s[24] // 2), (i // 2) ^ s[25], 0, 0),
                ),
                pl.BlockSpec((2, 256, 256), lambda i, s: (0, 0, 0)),
            ],
        ),
        out_shape=[
            jax.ShapeDtypeStruct((4, 2, 256, 256), F32),
            jax.ShapeDtypeStruct((2, 256, 256), F32),
        ],
        compiler_params=pltpu.CompilerParams(
            dimension_semantics=("arbitrary",), vmem_limit_bytes=48 * 2**20
        ),
    )(scal, blocks, *pieces, left)


def body(ancestors, panel_one, present_one, dinv_one, panel_two, present_two, dinv_two):
    row = lax.axis_index("row")
    col = lax.axis_index("col")
    zl, x, core = row // 8, (row // 2) % 4, row % 2
    zh, y = col // 4, col % 4
    first = core == 0

    with jax.named_scope("swap"):
        other_blocks = to_core(ancestors)
        rows_one = lax.dynamic_slice_in_dim(present_one, 4 * row, 4, 1)
        rows_two = lax.dynamic_slice_in_dim(present_two, 4 * row, 4, 1)
        masked_one = panel_one * rows_one[:, :, None, None].astype(BF16)
        masked_two = panel_two * rows_two[:, :, None, None].astype(BF16)
        mine = jnp.where(first, masked_one, masked_two)
        theirs = to_core(jnp.where(first, masked_two, masked_one))

    with jax.named_scope("gather"):
        pick = jnp.where(zh == core, mine, theirs)
        own = lax.dynamic_slice_in_dim(pick, y, 1, 1)[:, 0]
        own = to_plane(own)
        line = jnp.stack([own] + [to_zl(own, k) for k in (1, 2, 3)])
        pieces = [line] + [to_x(line, k) for k in (1, 2, 3)]

    present = jnp.where(first, present_one, present_two)
    order = jnp.array([[m, k] for m in range(4) for k in range(4)], jnp.int32)
    where = 4 * (x ^ order[:, 0]) + (zl ^ order[:, 1])

    def table(rows_of):
        live = lax.dynamic_slice_in_dim(present, 4 * rows_of, 4, 1)
        return jnp.concatenate(
            [where, jnp.transpose(live).reshape(8), jnp.stack([y, zh])]
        ).astype(jnp.int32)

    with jax.named_scope("product"):
        near, diag_near = products(table(row), ancestors, pieces, mine)
        far, diag_far = products(table(row ^ 1), other_blocks, pieces, theirs)

    def column(terms):
        total = terms[0]
        got = [to_y(terms[k].astype(SEND), k) for k in (1, 2, 3)]
        for value in got:
            total = total + value.astype(F32)
        return total[0] + to_zh(total[1])

    with jax.named_scope("near"):
        near = column(near)
    with jax.named_scope("far"):
        far = to_core(column(far))
    update_one = jnp.where(first, near, far)[None]
    update_two = jnp.where(first, far, near)[None]

    with jax.named_scope("diag"):
        diag = (diag_near + diag_far).reshape(4, 2, 64, 256)
        at = lambda k: lax.dynamic_index_in_dim(diag, y ^ k, 0, keepdims=False)
        part = at(0)
        for value in [to_y(at(k), k) for k in (1, 2, 3)]:
            part = part + value
        half = lambda k: lax.dynamic_index_in_dim(part, zh ^ k, 0, keepdims=False)
        piece = half(0) + to_zh(half(1))
        one, two, three = [to_x(piece, k) for k in (1, 2, 3)]
        piece = (piece + one) + (two + three)
        one, two, three = [to_zl(piece, k) for k in (1, 2, 3)]
        total = (piece + one) + (two + three)
        back = to_zh(total)
        pair = jnp.where(zh == 0, jnp.stack([total, back]), jnp.stack([back, total]))
        quarters = [pair] + [to_y(pair, k) for k in (1, 2, 3)]
        stack = jnp.stack(quarters)
        ordered = jnp.stack(
            [lax.dynamic_index_in_dim(stack, y ^ k, 0, keepdims=False) for k in range(4)]
        )
        whole = ordered.reshape(2, 256, 256)
        partner = to_core(whole)
        total_one = jnp.where(first, whole, partner)
        total_two = jnp.where(first, partner, whole)

    return (
        update_one,
        dinv_one.astype(F32) - total_one,
        update_two,
        dinv_two.astype(F32) - total_two,
    )


def solution(mesh):
    in_specs = (
        P("row", "col", None, None),
        P(None, "row", None, None),
        P(),
        P(),
        P(None, "row", None, None),
        P(),
        P(),
    )
    out_specs = (P(("row", "col"), None, None), P(), P(("row", "col"), None, None), P())
    return jax.shard_map(body, mesh=mesh, in_specs=in_specs, out_specs=out_specs, check_vma=False)
```

```python
import jax
import jax.numpy as jnp
from jax import lax
from jax.experimental import pallas as pl
from jax.experimental.pallas import tpu as pltpu
from jax.sharding import PartitionSpec as P

F32 = jnp.float32
BF16 = jnp.bfloat16
CODE = jnp.int16
AXES = ("row", "col")
PARTS = 2
WIDE = 256 // PARTS


def split_id(dev):
    row, col = dev // 8, dev % 8
    return row // 8, (row // 2) % 4, row % 2, col // 4, col % 4


def join_id(zl, x, core, zh, y):
    return ((zl * 4 + x) * 2 + core) * 8 + zh * 4 + y


def send(value, where):
    pairs = [(dev, join_id(*where(*split_id(dev)))) for dev in range(256)]
    return lax.ppermute(value, AXES, pairs)


def to_core(value):
    return send(value, lambda zl, x, core, zh, y: (zl, x, core ^ 1, zh, y))


def to_x(value, k):
    return send(value, lambda zl, x, core, zh, y: (zl, x ^ k, core, zh, y))


def along_x(value, k):
    return send(value, lambda zl, x, core, zh, y: (zl, (x + k) % 4, core, zh, y))


def to_zl(value, k):
    return send(value, lambda zl, x, core, zh, y: (zl ^ k, x, core, zh, y))


def to_y(value, k):
    return send(value, lambda zl, x, core, zh, y: (zl, x, core, zh, y ^ k))


def to_zh(value):
    return send(value, lambda zl, x, core, zh, y: (zl, x, core, zh ^ 1, y))


def plane_spot(zl, x, core, zh, y):
    h, bit = x % 2, y // 2
    x_to = (x + (2 * h - 1) * bit) % 4
    return 2 * zh + core, x_to, core ^ (y % 2), zl // 2, 2 * (zl % 2) + x // 2


def to_plane(value):
    return send(value, plane_spot)


def chunk_spot(zl, x, y):
    u = (x - 2 * (y % 2)) % 4
    h = jnp.where((u == 1) | (u == 2), 1, 0)
    bit = jnp.where(u >= 2, 1, 0)
    return 8 * h + 4 * (zl % 2) + 2 * (zl // 2) + bit


def encode(value):
    peak = jnp.max(jnp.abs(value), axis=0, keepdims=True)
    power = jnp.floor(jnp.log2(jnp.maximum(peak, 1e-30))) + 1.0
    scaled = jnp.round(value * jnp.exp2(15.0 - power))
    code = jnp.clip(scaled, -32767.0, 32767.0).astype(jnp.int32).astype(CODE)
    mark = jnp.broadcast_to(power, (16, value.shape[1])).astype(jnp.int32).astype(CODE)
    return code, mark


def decode(code, mark):
    return code.astype(jnp.int32).astype(F32) * jnp.exp2(mark.astype(jnp.int32).astype(F32) - 15.0)


def product_kernel(
    scal, near, far, p0, p1, p2, p3, p4, left_near, left_far, own, q1, q2, q3, diag_ref, wide
):
    step = pl.program_id(0)

    @pl.when(step == 0)
    def _():
        diag_ref[...] = jnp.zeros_like(diag_ref)
        for m, piece in enumerate((p0, p1, p2)):
            for z in range(4):
                at = pl.multiple_of(scal[4 * m + z] * 256, 256)
                for k in range(2):
                    wide[pl.ds(at, 256), k * WIDE : (k + 1) * WIDE] = piece[k, z]
        for k, piece in enumerate((p3, p4)):
            for z in range(4):
                at = pl.multiple_of(scal[12 + z] * 256, 256)
                wide[pl.ds(at, 256), k * WIDE : (k + 1) * WIDE] = piece[z]

    half = lax.rem(step, 4) // 2
    zrel = half ^ scal[33]
    side = step // 4

    def work(blocks, left):
        acc = jnp.zeros((256, 2 * WIDE), F32)
        for j in range(16):
            acc += jnp.dot(
                blocks[0, j], wide[j * 256 : (j + 1) * 256, :], preferred_element_type=F32
            )
        for k in range(2):
            live = (-scal[16 + 2 * step + k]).astype(F32)
            term = acc[:, k * WIDE : (k + 1) * WIDE] * live
            high = term.astype(BF16)
            rest = (term - high.astype(F32)).astype(BF16)
            both = jnp.dot(
                left[k, 0], jnp.concatenate([high, rest], axis=1), preferred_element_type=F32
            )
            diag_ref[k] += both[:, :WIDE] + both[:, WIDE:]
            to = (2 * lax.rem(step, 2) + k) ^ scal[32]

            @pl.when(to == 0)
            def _():
                own[zrel, side] = term

            @pl.when(to != 0)
            def _():
                code, mark = encode(term)
                for m, ref in ((1, q1), (2, q2), (3, q3)):

                    @pl.when(to == m)
                    def _():
                        ref[zrel, side, 0:256] = code
                        ref[zrel, side, 256:272] = mark

    @pl.when(step < 4)
    def _():
        work(near, left_near)

    @pl.when(step >= 4)
    def _():
        work(far, left_far)


def total_kernel(own, q1, q2, q3, keep, give):
    for z in range(2):
        for side in range(2):
            value = own[z, side]
            for ref in (q1, q2, q3):
                value += decode(ref[z, side, 0:256], ref[z, side, 256:257])
            if z == 0:
                keep[side] = value
            else:
                code, mark = encode(value)
                give[side, 0:256] = code
                give[side, 256:272] = mark


def totals(own, others):
    return pl.pallas_call(
        total_kernel,
        out_shape=[
            jax.ShapeDtypeStruct((2, 256, WIDE), F32),
            jax.ShapeDtypeStruct((2, 272, WIDE), CODE),
        ],
        compiler_params=pltpu.CompilerParams(vmem_limit_bytes=32 * 2**20),
    )(own, *others)


def products(scal, near, far, pieces, left_near, left_far):
    early = lambda i: jnp.minimum(i, 3)
    late = lambda i: jnp.maximum(i - 4, 0)
    full = lambda shape: pl.BlockSpec(shape, lambda i, s: (0,) * len(shape))
    return pl.pallas_call(
        product_kernel,
        grid_spec=pltpu.PrefetchScalarGridSpec(
            num_scalar_prefetch=1,
            grid=(8,),
            in_specs=[
                pl.BlockSpec((1, 16, 256, 256), lambda i, s: (early(i), 0, 0, 0)),
                pl.BlockSpec((1, 16, 256, 256), lambda i, s: (late(i), 0, 0, 0)),
            ]
            + [full(p.shape) for p in pieces]
            + [
                pl.BlockSpec((2, 1, 256, 256), lambda i, s: (0, early(i), 0, 0)),
                pl.BlockSpec((2, 1, 256, 256), lambda i, s: (0, late(i), 0, 0)),
            ],
            out_specs=[
                full((2, 2, 256, WIDE)),
                full((2, 2, 272, WIDE)),
                full((2, 2, 272, WIDE)),
                full((2, 2, 272, WIDE)),
                full((2, 256, WIDE)),
            ],
            scratch_shapes=[pltpu.VMEM((4096, 2 * WIDE), BF16)],
        ),
        out_shape=[jax.ShapeDtypeStruct((2, 2, 256, WIDE), F32)]
        + [jax.ShapeDtypeStruct((2, 2, 272, WIDE), CODE)] * 3
        + [jax.ShapeDtypeStruct((2, 256, WIDE), F32)],
        cost_estimate=pl.CostEstimate(
            flops=2 * 2048 * 4096 * 2 * WIDE, transcendentals=0, bytes_accessed=24 * 2**20
        ),
        compiler_params=pltpu.CompilerParams(
            dimension_semantics=("arbitrary",), vmem_limit_bytes=48 * 2**20
        ),
    )(scal, near, far, *pieces, left_near, left_far)


def body(ancestors, panel_one, present_one, dinv_one, panel_two, present_two, dinv_two):
    row = lax.axis_index("row")
    col = lax.axis_index("col")
    zl, x, core = row // 8, (row // 2) % 4, row % 2
    zh, y = col // 4, col % 4
    first = core == 0
    rows_one = lax.dynamic_slice_in_dim(present_one, 4 * row, 4, 1)
    rows_two = lax.dynamic_slice_in_dim(present_two, 4 * row, 4, 1)

    with jax.named_scope("spread"):
        take = lambda value: lax.dynamic_slice_in_dim(value, 2 * zh + y // 2, 1, 1)
        one, two = take(panel_one)[:, 0], take(panel_two)[:, 0]
        live_one, live_two = take(rows_one), take(rows_two)
        chosen = core == y % 2
        live = jnp.where(chosen, live_one, live_two).astype(BF16)
        own = jnp.where(chosen, one, two) * live[:, :, None]
        shares = [to_plane(own[:, :, h * WIDE : (h + 1) * WIDE]) for h in range(PARTS)]

    with jax.named_scope("swap"):
        masked_one = panel_one * rows_one[:, :, None, None].astype(BF16)
        masked_two = panel_two * rows_two[:, :, None, None].astype(BF16)
        mine = jnp.swapaxes(jnp.where(first, masked_one, masked_two), 2, 3)
        theirs = to_core(jnp.swapaxes(jnp.where(first, masked_two, masked_one), 2, 3))
        other_blocks = to_core(ancestors)

    present = jnp.where(first, present_one, present_two)
    x_from = ((x + jnp.array([0, 3, 1, 2], jnp.int32)) % 4)[:, None]
    z_from = (zl ^ jnp.arange(4, dtype=jnp.int32))[None, :]
    spots = chunk_spot(z_from, x_from, y)
    live_near = lax.dynamic_slice_in_dim(present, 4 * row, 4, 1)
    live_far = lax.dynamic_slice_in_dim(present, 4 * (row ^ 1), 4, 1)
    scal = jnp.concatenate(
        [
            spots.reshape(16),
            jnp.transpose(live_near).reshape(8),
            jnp.transpose(live_far).reshape(8),
            jnp.stack([y, zh]),
        ]
    ).astype(jnp.int32)

    def tie(value, *others):
        return lax.optimization_barrier((value, *others))[0]

    def line_of(share):
        return jnp.stack([share] + [to_zl(share, k) for k in (1, 2, 3)], axis=1)

    def over_y(out):
        return out[0], [to_y(out[m], m) for m in (1, 2, 3)]

    with jax.named_scope("gather0"):
        line = line_of(shares[0])
        before, after = along_x(line, 1), along_x(line, -1)
        low, high = before[0], after[1]
        pieces = [line, before, after, along_x(low, 1), along_x(high, -1)]
    with jax.named_scope("product0"):
        out_a = products(scal, ancestors, other_blocks, pieces, mine, theirs)
    with jax.named_scope("column0"):
        sent_a = over_y(out_a)
    with jax.named_scope("gather1"):
        line = tie(line_of(shares[1]), low, high)
        before, after = along_x(line, 1), along_x(line, -1)
        pieces = [line, before, after, along_x(before[0], 1), along_x(after[1], -1)]
    with jax.named_scope("product1"):
        pieces[0] = tie(pieces[0], out_a[4])
        out_b = products(scal, ancestors, other_blocks, pieces, mine, theirs)
    with jax.named_scope("total0"):
        keep_a, give_a = totals(sent_a[0], [tie(v, out_b[4]) for v in sent_a[1]])
    with jax.named_scope("diag_y"):
        diag = jnp.concatenate([out_a[4], tie(out_b[4], keep_a)], axis=2).reshape(4, 128, 256)
        at = lambda k: lax.dynamic_index_in_dim(diag, y ^ k, 0, keepdims=False)
        got = [to_y(at(k), k) for k in (1, 2, 3)]
        part = (at(0) + got[0]) + (got[1] + got[2])
    with jax.named_scope("column1"):
        sent_b = over_y(out_b)
    with jax.named_scope("diag_z"):
        one, two, three = [to_zl(part, k) for k in (1, 2, 3)]
        part = (part + one) + (two + three)
        part = part + to_zh(part)
    with jax.named_scope("total1"):
        keep_b, give_b = totals(*sent_b)
        got = to_zh(jnp.concatenate([give_a, give_b], axis=2))
        keep = jnp.concatenate([keep_a, keep_b], axis=2)
        block = keep + decode(got[:, :256], got[:, 256:257])
    with jax.named_scope("diag_x"):
        part = tie(part, keep_b)
        one, two, three = [to_x(part, k) for k in (1, 2, 3)]
        part = (part + one) + (two + three)
    with jax.named_scope("diag_back"):
        stack = jnp.stack([part] + [to_y(part, k) for k in (1, 2, 3)])
        ordered = [lax.dynamic_index_in_dim(stack, y ^ k, 0, keepdims=False) for k in range(4)]
        whole = jnp.stack(ordered).reshape(2, 256, 256)
        partner = to_core(jnp.concatenate([whole, block[1:]]))
    near, far = block[0], partner[2]
    return (
        jnp.where(first, near, far)[None],
        dinv_one.astype(F32) - jnp.where(first, whole, partner[:2]),
        jnp.where(first, far, near)[None],
        dinv_two.astype(F32) - jnp.where(first, partner[:2], whole),
    )


def solution(mesh):
    in_specs = (
        P("row", "col", None, None),
        P(None, "row", None, None),
        P(),
        P(),
        P(None, "row", None, None),
        P(),
        P(),
    )
    out_specs = (P(("row", "col"), None, None), P(), P(("row", "col"), None, None), P())
    return jax.shard_map(body, mesh=mesh, in_specs=in_specs, out_specs=out_specs, check_vma=False)
```

```python
import jax
import jax.numpy as jnp
from jax import lax
from jax.experimental import pallas as pl
from jax.experimental.pallas import tpu as pltpu
from jax.sharding import PartitionSpec as P

F32 = jnp.float32
BF16 = jnp.bfloat16
CODE = jnp.int16
AXES = ("row", "col")


def split_id(dev):
    row, col = dev // 8, dev % 8
    return row // 8, (row // 2) % 4, row % 2, col // 4, col % 4


def join_id(zl, x, core, zh, y):
    return ((zl * 4 + x) * 2 + core) * 8 + zh * 4 + y


def send(value, where):
    pairs = [(dev, join_id(*where(*split_id(dev)))) for dev in range(256)]
    return lax.ppermute(value, AXES, pairs)


def to_core(value):
    return send(value, lambda zl, x, core, zh, y: (zl, x, core ^ 1, zh, y))


def to_x(value, k):
    return send(value, lambda zl, x, core, zh, y: (zl, x ^ k, core, zh, y))


def along_x(value, k):
    return send(value, lambda zl, x, core, zh, y: (zl, (x + k) % 4, core, zh, y))


def to_zl(value, k):
    return send(value, lambda zl, x, core, zh, y: (zl ^ k, x, core, zh, y))


def to_y(value, k):
    return send(value, lambda zl, x, core, zh, y: (zl, x, core, zh, y ^ k))


def to_zh(value):
    return send(value, lambda zl, x, core, zh, y: (zl, x, core, zh ^ 1, y))


def plane_spot(zl, x, core, zh, y):
    h, bit = x % 2, y // 2
    x_to = (x + (2 * h - 1) * bit) % 4
    z_to = 2 * (zh ^ (zl // 2) ^ (zl % 2)) + (core ^ (zl // 2))
    return z_to, x_to, core ^ (y % 2), zl // 2, 2 * (zl % 2) + x // 2


def to_plane(value):
    return send(value, plane_spot)


def chunk_spot(zl, x, zh, y):
    u = (x - 2 * (y % 2)) % 4
    h = jnp.where((u == 1) | (u == 2), 1, 0)
    bit = jnp.where(u >= 2, 1, 0)
    return 8 * h + 4 * ((zl % 2) ^ zh) + 2 * ((zl // 2) ^ zh ^ (y // 2)) + bit


def encode(value):
    peak = jnp.max(jnp.abs(value), axis=0, keepdims=True)
    power = jnp.floor(jnp.log2(jnp.maximum(peak, 1e-30))) + 1.0
    scaled = jnp.round(value * jnp.exp2(15.0 - power))
    code = jnp.clip(scaled, -32767.0, 32767.0).astype(jnp.int32).astype(CODE)
    mark = jnp.broadcast_to(power, (16, value.shape[1])).astype(jnp.int32).astype(CODE)
    return code, mark


def decode(code, mark):
    return code.astype(jnp.int32).astype(F32) * jnp.exp2(mark.astype(jnp.int32).astype(F32) - 15.0)


def first_kernel(scal, near, far, a0, b0, a1, b1, a2, b2, acc_ref, wide):
    step = pl.program_id(0)

    @pl.when(step == 0)
    def _():
        for k, group in enumerate(((a0, a1, a2), (b0, b1, b2))):
            for m, piece in enumerate(group):
                for z in range(4):
                    at = (4 * m + z) * 256
                    live = scal[34 + 2 * scal[4 * m + z] + k] > 0
                    value = jnp.where(live, piece[z], jnp.zeros((256, 256), BF16))
                    wide[at : at + 256, k * 256 : (k + 1) * 256] = value

    def work(blocks):
        acc = jnp.zeros((256, 512), F32)
        for pos in range(12):
            acc += jnp.dot(
                blocks[0, scal[pos]],
                wide[pos * 256 : (pos + 1) * 256, :],
                preferred_element_type=F32,
            )
        acc_ref[0] = acc

    @pl.when(step < 4)
    def _():
        work(near)

    @pl.when(step >= 4)
    def _():
        work(far)


def second_kernel(
    scal, acc_in, near, far, a3, b3, left_near, left_far, own, q1, q2, q3, diag_ref, wide
):
    step = pl.program_id(0)

    @pl.when(step == 0)
    def _():
        diag_ref[...] = jnp.zeros_like(diag_ref)
        for k, piece in enumerate((a3, b3)):
            for z in range(4):
                live = scal[34 + 2 * scal[12 + z] + k] > 0
                value = jnp.where(live, piece[z], jnp.zeros((256, 256), BF16))
                wide[z * 256 : (z + 1) * 256, k * 256 : (k + 1) * 256] = value

    half = lax.rem(step, 4) // 2
    zrel = half ^ scal[33]
    side = step // 4

    def work(blocks, left):
        acc = acc_in[0]
        for z in range(4):
            acc += jnp.dot(
                blocks[0, scal[12 + z] & 7],
                wide[z * 256 : (z + 1) * 256, :],
                preferred_element_type=F32,
            )
        for k in range(2):
            live = (-scal[16 + 2 * step + k]).astype(F32)
            term = acc[:, k * 256 : (k + 1) * 256] * live
            high = term.astype(BF16)
            rest = (term - high.astype(F32)).astype(BF16)
            both = jnp.concatenate([high, rest], axis=1)
            both = jnp.dot(left[k, 0], both, preferred_element_type=F32)
            diag_ref[k] += both[:, :256] + both[:, 256:]
            to = (2 * lax.rem(step, 2) + k) ^ scal[32]

            @pl.when(to == 0)
            def _():
                own[zrel, side] = term

            @pl.when(to != 0)
            def _():
                code, mark = encode(term)
                for m, ref in ((1, q1), (2, q2), (3, q3)):

                    @pl.when(to == m)
                    def _():
                        ref[zrel, side, 0:256] = code
                        ref[zrel, side, 256:272] = mark

    @pl.when(step < 4)
    def _():
        work(near, left_near)

    @pl.when(step >= 4)
    def _():
        work(far, left_far)


def early(i):
    return jnp.minimum(i, 3)


def late(i):
    return jnp.maximum(i - 4, 0)


def full(shape):
    return pl.BlockSpec(shape, lambda i, s: (0,) * len(shape))


PARAMS = pltpu.CompilerParams(dimension_semantics=("arbitrary",), vmem_limit_bytes=48 * 2**20)


def first_products(scal, near, far, pieces):
    return pl.pallas_call(
        first_kernel,
        grid_spec=pltpu.PrefetchScalarGridSpec(
            num_scalar_prefetch=1,
            grid=(8,),
            in_specs=[
                pl.BlockSpec((1, 16, 256, 256), lambda i, s: (early(i), 0, 0, 0)),
                pl.BlockSpec((1, 16, 256, 256), lambda i, s: (late(i), 0, 0, 0)),
            ]
            + [full(p.shape) for p in pieces],
            out_specs=pl.BlockSpec((1, 256, 512), lambda i, s: (i, 0, 0)),
            scratch_shapes=[pltpu.VMEM((3072, 512), BF16)],
        ),
        out_shape=jax.ShapeDtypeStruct((8, 256, 512), F32),
        cost_estimate=pl.CostEstimate(
            flops=2 * 2048 * 3072 * 512, transcendentals=0, bytes_accessed=24 * 2**20
        ),
        compiler_params=PARAMS,
    )(scal, near, far, *pieces)


def second_products(scal, acc, near, far, pieces, left_near, left_far):
    return pl.pallas_call(
        second_kernel,
        grid_spec=pltpu.PrefetchScalarGridSpec(
            num_scalar_prefetch=1,
            grid=(8,),
            in_specs=[
                pl.BlockSpec((1, 256, 512), lambda i, s: (i, 0, 0)),
                pl.BlockSpec((1, 8, 256, 256), lambda i, s: (early(i), s[12] // 8, 0, 0)),
                pl.BlockSpec((1, 8, 256, 256), lambda i, s: (late(i), s[12] // 8, 0, 0)),
            ]
            + [full(p.shape) for p in pieces]
            + [
                pl.BlockSpec((2, 1, 256, 256), lambda i, s: (0, early(i), 0, 0)),
                pl.BlockSpec((2, 1, 256, 256), lambda i, s: (0, late(i), 0, 0)),
            ],
            out_specs=[
                full((2, 2, 256, 256)),
                full((2, 2, 272, 256)),
                full((2, 2, 272, 256)),
                full((2, 2, 272, 256)),
                full((2, 256, 256)),
            ],
            scratch_shapes=[pltpu.VMEM((1024, 512), BF16)],
        ),
        out_shape=[jax.ShapeDtypeStruct((2, 2, 256, 256), F32)]
        + [jax.ShapeDtypeStruct((2, 2, 272, 256), CODE)] * 3
        + [jax.ShapeDtypeStruct((2, 256, 256), F32)],
        cost_estimate=pl.CostEstimate(
            flops=2 * 2048 * 1024 * 512, transcendentals=0, bytes_accessed=16 * 2**20
        ),
        compiler_params=PARAMS,
    )(scal, acc, near, far, *pieces, left_near, left_far)


def total_kernel(own, q1, q2, q3, keep, give):
    for z in range(2):
        for side in range(2):
            value = own[z, side]
            for ref in (q1, q2, q3):
                value += decode(ref[z, side, 0:256], ref[z, side, 256:257])
            if z == 0:
                keep[side] = value
            else:
                code, mark = encode(value)
                give[side, 0:256] = code
                give[side, 256:272] = mark


def totals(own, others):
    return pl.pallas_call(
        total_kernel,
        out_shape=[
            jax.ShapeDtypeStruct((2, 256, 256), F32),
            jax.ShapeDtypeStruct((2, 272, 256), CODE),
        ],
        compiler_params=pltpu.CompilerParams(vmem_limit_bytes=32 * 2**20),
    )(own, *others)


def products(scal, near, far, pieces, left_near, left_far):
    early = lambda i: jnp.minimum(i, 3)
    late = lambda i: jnp.maximum(i - 4, 0)
    full = lambda shape: pl.BlockSpec(shape, lambda i, s: (0,) * len(shape))
    return pl.pallas_call(
        product_kernel,
        grid_spec=pltpu.PrefetchScalarGridSpec(
            num_scalar_prefetch=1,
            grid=(8,),
            in_specs=[
                pl.BlockSpec((1, 16, 256, 256), lambda i, s: (early(i), 0, 0, 0)),
                pl.BlockSpec((1, 16, 256, 256), lambda i, s: (late(i), 0, 0, 0)),
            ]
            + [full(p.shape) for p in pieces]
            + [
                pl.BlockSpec((2, 1, 256, 256), lambda i, s: (0, early(i), 0, 0)),
                pl.BlockSpec((2, 1, 256, 256), lambda i, s: (0, late(i), 0, 0)),
            ],
            out_specs=[
                full((2, 2, 256, 256)),
                full((2, 2, 272, 256)),
                full((2, 2, 272, 256)),
                full((2, 2, 272, 256)),
                full((2, 256, 256)),
            ],
            scratch_shapes=[pltpu.VMEM((4096, 2 * 256), BF16)],
        ),
        out_shape=[jax.ShapeDtypeStruct((2, 2, 256, 256), F32)]
        + [jax.ShapeDtypeStruct((2, 2, 272, 256), CODE)] * 3
        + [jax.ShapeDtypeStruct((2, 256, 256), F32)],
        cost_estimate=pl.CostEstimate(
            flops=2 * 2048 * 4096 * 2 * 256, transcendentals=0, bytes_accessed=24 * 2**20
        ),
        compiler_params=pltpu.CompilerParams(
            dimension_semantics=("arbitrary",), vmem_limit_bytes=48 * 2**20
        ),
    )(scal, near, far, *pieces, left_near, left_far)


def body(ancestors, panel_one, present_one, dinv_one, panel_two, present_two, dinv_two):
    row = lax.axis_index("row")
    col = lax.axis_index("col")
    zl, x, core = row // 8, (row // 2) % 4, row % 2
    zh, y = col // 4, col % 4
    first = core == 0
    tie = lambda *values: lax.optimization_barrier(values)

    with jax.named_scope("spread"):
        take = lambda value: lax.dynamic_index_in_dim(value, 2 * zh + y // 2, 1, keepdims=False)
        own = to_plane(jnp.where(core == y % 2, take(panel_one), take(panel_two)))

    with jax.named_scope("swap"):
        other_blocks = to_core(ancestors)
        held_one, held_two, own = tie(panel_one, panel_two, own)
        mine = jnp.swapaxes(jnp.where(first, held_one, held_two), 2, 3)
        theirs = to_core(jnp.swapaxes(jnp.where(first, held_two, held_one), 2, 3))

    present = jnp.where(first, present_one, present_two)
    x_from = ((x + jnp.array([0, 3, 1, 2], jnp.int32)) % 4)[:, None]
    z_from = (zl ^ jnp.arange(4, dtype=jnp.int32))[None, :]
    spots = chunk_spot(z_from, x_from, zh, y)
    live_near = lax.dynamic_slice_in_dim(present, 4 * row, 4, 1)
    live_far = lax.dynamic_slice_in_dim(present, 4 * (row ^ 1), 4, 1)
    scal = jnp.concatenate(
        [
            spots.reshape(16),
            jnp.transpose(live_near).reshape(8),
            jnp.transpose(live_far).reshape(8),
            jnp.stack([y, zh]),
            jnp.transpose(lax.dynamic_slice_in_dim(present, 16 * col, 16, 1)).reshape(32),
        ]
    ).astype(jnp.int32)

    with jax.named_scope("gather"):
        parts = [own] + [to_zl(own, k) for k in (1, 2, 3)]
        a0, b0 = [jnp.stack([part[k] for part in parts]) for k in range(2)]
        a0, b0, other_blocks, theirs = tie(a0, b0, other_blocks, theirs)
        a1, b2 = along_x(a0, 1), along_x(b0, -1)
        b1, a2 = along_x(b0, 1), along_x(a0, -1)
        a3, b3 = along_x(a1, 1), along_x(b2, -1)
    with jax.named_scope("product"):
        acc = first_products(scal, ancestors, other_blocks, [a0, b0, a1, b1, a2, b2])
        out = second_products(scal, acc, ancestors, other_blocks, [a3, b3], mine, theirs)

    def shares(value, spot, move):
        at = lambda k: lax.dynamic_index_in_dim(value, spot ^ k, 0, keepdims=False)
        one, two, three = [move(at(k), k) for k in (1, 2, 3)]
        return (at(0) + one) + (two + three)

    def collect(value, spot, move):
        stack = jnp.stack([value] + [move(value, k) for k in (1, 2, 3)])
        return jnp.stack(
            [lax.dynamic_index_in_dim(stack, spot ^ k, 0, keepdims=False) for k in range(4)]
        )

    with jax.named_scope("diag"):
        piece = shares(out[4].reshape(4, 128, 256), y, to_y)
        piece = shares(piece.reshape(4, 32, 256), x, to_x)
        one, two, three = [to_zl(piece, k) for k in (1, 2, 3)]
        piece = (piece + one) + (two + three)
        piece = piece + to_zh(piece)
    with jax.named_scope("column"):
        keep, give = totals(out[0], [to_y(out[m], m) for m in (1, 2, 3)])
        got = to_zh(give)
        block = keep + decode(got[:, :256], got[:, 256:257])
    with jax.named_scope("back"):
        piece = tie(piece, keep)[0]
        part = collect(piece, x, to_x).reshape(128, 256)
        whole = collect(part, y, to_y).reshape(2, 256, 256)
        near, far = block[0], to_core(block[1])
        whole = tie(whole, far)[0]
        partner = to_core(whole)
    return (
        jnp.where(first, near, far)[None],
        dinv_one.astype(F32) - jnp.where(first, whole, partner),
        jnp.where(first, far, near)[None],
        dinv_two.astype(F32) - jnp.where(first, partner, whole),
    )


def solution(mesh):
    in_specs = (
        P("row", "col", None, None),
        P(None, "row", None, None),
        P(),
        P(),
        P(None, "row", None, None),
        P(),
        P(),
    )
    out_specs = (P(("row", "col"), None, None), P(), P(("row", "col"), None, None), P())
    return jax.shard_map(body, mesh=mesh, in_specs=in_specs, out_specs=out_specs, check_vma=False)
```

```python
import jax
import jax.numpy as jnp
from jax import lax
from jax.experimental import pallas as pl
from jax.experimental.pallas import tpu as pltpu
from jax.sharding import PartitionSpec as P

F32 = jnp.float32
BF16 = jnp.bfloat16
CODE = jnp.int16
AXES = ("row", "col")


def split_id(dev):
    row, col = dev // 8, dev % 8
    return row // 8, (row // 2) % 4, row % 2, col // 4, col % 4


def join_id(zl, x, core, zh, y):
    return ((zl * 4 + x) * 2 + core) * 8 + zh * 4 + y


def send(value, where):
    pairs = [(dev, join_id(*where(*split_id(dev)))) for dev in range(256)]
    return lax.ppermute(value, AXES, pairs)


def to_core(value):
    return send(value, lambda zl, x, core, zh, y: (zl, x, core ^ 1, zh, y))


def to_x(value, k):
    return send(value, lambda zl, x, core, zh, y: (zl, x ^ k, core, zh, y))


def along_x(value, k):
    return send(value, lambda zl, x, core, zh, y: (zl, (x + k) % 4, core, zh, y))


def to_zl(value, k):
    return send(value, lambda zl, x, core, zh, y: (zl ^ k, x, core, zh, y))


def to_y(value, k):
    return send(value, lambda zl, x, core, zh, y: (zl, x, core, zh, y ^ k))


def to_zh(value):
    return send(value, lambda zl, x, core, zh, y: (zl, x, core, zh ^ 1, y))


def plane_spot(zl, x, core, zh, y):
    h, bit = x % 2, y // 2
    x_to = (x + (2 * h - 1) * bit) % 4
    z_to = 2 * (zh ^ (zl // 2) ^ (zl % 2)) + (core ^ (zl // 2))
    return z_to, x_to, core ^ (y % 2), zl // 2, 2 * (zl % 2) + x // 2


def to_plane(value):
    return send(value, plane_spot)


def chunk_spot(zl, x, zh, y):
    u = (x - 2 * (y % 2)) % 4
    h = jnp.where((u == 1) | (u == 2), 1, 0)
    bit = jnp.where(u >= 2, 1, 0)
    return 8 * h + 4 * ((zl % 2) ^ zh) + 2 * ((zl // 2) ^ zh ^ (y // 2)) + bit


def encode(value):
    peak = jnp.max(jnp.abs(value), axis=0, keepdims=True)
    power = jnp.floor(jnp.log2(jnp.maximum(peak, 1e-30))) + 1.0
    scaled = jnp.round(value * jnp.exp2(15.0 - power))
    code = jnp.clip(scaled, -32767.0, 32767.0).astype(jnp.int32).astype(CODE)
    mark = jnp.broadcast_to(power, (16, value.shape[1])).astype(jnp.int32).astype(CODE)
    return code, mark


def decode(code, mark):
    return code.astype(jnp.int32).astype(F32) * jnp.exp2(mark.astype(jnp.int32).astype(F32) - 15.0)


def first_kernel(scal, near, far, a0, b0, a1, b1, a2, b2, acc_ref, wide):
    step = pl.program_id(0)

    @pl.when(step == 0)
    def _():
        for k, group in enumerate(((a0, a1, a2), (b0, b1, b2))):
            for m, piece in enumerate(group):
                for z in range(4):
                    at = (4 * m + z) * 256
                    live = scal[34 + 2 * scal[4 * m + z] + k] > 0
                    value = jnp.where(live, piece[z], jnp.zeros((256, 256), BF16))
                    wide[at : at + 256, k * 256 : (k + 1) * 256] = value

    for side, blocks in enumerate((near, far)):
        acc = jnp.zeros((256, 512), F32)
        for pos in range(12):
            acc += jnp.dot(
                blocks[0, scal[pos]],
                wide[pos * 256 : (pos + 1) * 256, :],
                preferred_element_type=F32,
            )
        acc_ref[side, 0] = acc


def second_kernel(
    scal, acc_in, near, far, a3, b3, left_near, left_far, own, q1, q2, q3, diag_ref, wide
):
    step = pl.program_id(0)

    @pl.when(step == 0)
    def _():
        diag_ref[...] = jnp.zeros_like(diag_ref)
        for k, piece in enumerate((a3, b3)):
            for z in range(4):
                live = scal[34 + 2 * scal[12 + z] + k] > 0
                value = jnp.where(live, piece[z], jnp.zeros((256, 256), BF16))
                wide[z * 256 : (z + 1) * 256, k * 256 : (k + 1) * 256] = value

    zrel = (step // 2) ^ scal[33]
    for side, (blocks, left) in enumerate(((near, left_near), (far, left_far))):
        acc = acc_in[side, 0]
        for z in range(4):
            acc += jnp.dot(
                blocks[0, scal[12 + z] & 7],
                wide[z * 256 : (z + 1) * 256, :],
                preferred_element_type=F32,
            )
        for k in range(2):
            live = (-scal[16 + 8 * side + 2 * step + k]).astype(F32)
            term = acc[:, k * 256 : (k + 1) * 256] * live
            high = term.astype(BF16)
            rest = (term - high.astype(F32)).astype(BF16)
            both = jnp.concatenate([high, rest], axis=1)
            both = jnp.dot(left[k, 0], both, preferred_element_type=F32)
            diag_ref[k] += both[:, :256] + both[:, 256:]
            code, mark = encode(term)
            to = (2 * lax.rem(step, 2) + k) ^ scal[32]

            @pl.when(to == 0)
            def _():
                own[zrel, side] = term

            for m, ref in ((1, q1), (2, q2), (3, q3)):

                @pl.when(to == m)
                def _():
                    ref[zrel, side, 0:256] = code
                    ref[zrel, side, 256:272] = mark


def full(shape):
    return pl.BlockSpec(shape, lambda i, s: (0,) * len(shape))


PARAMS = pltpu.CompilerParams(dimension_semantics=("arbitrary",), vmem_limit_bytes=48 * 2**20)


def first_products(scal, near, far, pieces):
    return pl.pallas_call(
        first_kernel,
        grid_spec=pltpu.PrefetchScalarGridSpec(
            num_scalar_prefetch=1,
            grid=(4,),
            in_specs=[
                pl.BlockSpec((1, 16, 256, 256), lambda i, s: (i, 0, 0, 0)),
                pl.BlockSpec((1, 16, 256, 256), lambda i, s: (i, 0, 0, 0)),
            ]
            + [full(p.shape) for p in pieces],
            out_specs=pl.BlockSpec((2, 1, 256, 512), lambda i, s: (0, i, 0, 0)),
            scratch_shapes=[pltpu.VMEM((3072, 512), BF16)],
        ),
        out_shape=jax.ShapeDtypeStruct((2, 4, 256, 512), F32),
        cost_estimate=pl.CostEstimate(
            flops=2 * 2048 * 3072 * 512, transcendentals=0, bytes_accessed=24 * 2**20
        ),
        compiler_params=PARAMS,
    )(scal, near, far, *pieces)


def second_products(scal, acc, near, far, pieces, left_near, left_far):
    return pl.pallas_call(
        second_kernel,
        grid_spec=pltpu.PrefetchScalarGridSpec(
            num_scalar_prefetch=1,
            grid=(4,),
            in_specs=[
                pl.BlockSpec((2, 1, 256, 512), lambda i, s: (0, i, 0, 0)),
                pl.BlockSpec((1, 8, 256, 256), lambda i, s: (i, s[12] // 8, 0, 0)),
                pl.BlockSpec((1, 8, 256, 256), lambda i, s: (i, s[12] // 8, 0, 0)),
            ]
            + [full(p.shape) for p in pieces]
            + [
                pl.BlockSpec((2, 1, 256, 256), lambda i, s: (0, i, 0, 0)),
                pl.BlockSpec((2, 1, 256, 256), lambda i, s: (0, i, 0, 0)),
            ],
            out_specs=[
                full((2, 2, 256, 256)),
                full((2, 2, 272, 256)),
                full((2, 2, 272, 256)),
                full((2, 2, 272, 256)),
                full((2, 256, 256)),
            ],
            scratch_shapes=[pltpu.VMEM((1024, 512), BF16)],
        ),
        out_shape=[jax.ShapeDtypeStruct((2, 2, 256, 256), F32)]
        + [jax.ShapeDtypeStruct((2, 2, 272, 256), CODE)] * 3
        + [jax.ShapeDtypeStruct((2, 256, 256), F32)],
        cost_estimate=pl.CostEstimate(
            flops=2 * 2048 * 1024 * 512, transcendentals=0, bytes_accessed=16 * 2**20
        ),
        compiler_params=PARAMS,
    )(scal, acc, near, far, *pieces, left_near, left_far)


def total_kernel(own, q1, q2, q3, keep, give):
    for z in range(2):
        for side in range(2):
            value = own[z, side]
            for ref in (q1, q2, q3):
                value += decode(ref[z, side, 0:256], ref[z, side, 256:257])
            if z == 0:
                keep[side] = value
            else:
                code, mark = encode(value)
                give[side, 0:256] = code
                give[side, 256:272] = mark


def totals(own, others):
    return pl.pallas_call(
        total_kernel,
        out_shape=[
            jax.ShapeDtypeStruct((2, 256, 256), F32),
            jax.ShapeDtypeStruct((2, 272, 256), CODE),
        ],
        compiler_params=pltpu.CompilerParams(vmem_limit_bytes=32 * 2**20),
    )(own, *others)


def products(scal, near, far, pieces, left_near, left_far):
    early = lambda i: jnp.minimum(i, 3)
    late = lambda i: jnp.maximum(i - 4, 0)
    full = lambda shape: pl.BlockSpec(shape, lambda i, s: (0,) * len(shape))
    return pl.pallas_call(
        product_kernel,
        grid_spec=pltpu.PrefetchScalarGridSpec(
            num_scalar_prefetch=1,
            grid=(4,),
            in_specs=[
                pl.BlockSpec((1, 16, 256, 256), lambda i, s: (i, 0, 0, 0)),
                pl.BlockSpec((1, 16, 256, 256), lambda i, s: (i, 0, 0, 0)),
            ]
            + [full(p.shape) for p in pieces]
            + [
                pl.BlockSpec((2, 1, 256, 256), lambda i, s: (0, i, 0, 0)),
                pl.BlockSpec((2, 1, 256, 256), lambda i, s: (0, i, 0, 0)),
            ],
            out_specs=[
                full((2, 2, 256, 256)),
                full((2, 2, 272, 256)),
                full((2, 2, 272, 256)),
                full((2, 2, 272, 256)),
                full((2, 256, 256)),
            ],
            scratch_shapes=[pltpu.VMEM((4096, 2 * 256), BF16)],
        ),
        out_shape=[jax.ShapeDtypeStruct((2, 2, 256, 256), F32)]
        + [jax.ShapeDtypeStruct((2, 2, 272, 256), CODE)] * 3
        + [jax.ShapeDtypeStruct((2, 256, 256), F32)],
        cost_estimate=pl.CostEstimate(
            flops=2 * 2048 * 4096 * 2 * 256, transcendentals=0, bytes_accessed=24 * 2**20
        ),
        compiler_params=pltpu.CompilerParams(
            dimension_semantics=("arbitrary",), vmem_limit_bytes=48 * 2**20
        ),
    )(scal, near, far, *pieces, left_near, left_far)


def body(ancestors, panel_one, present_one, dinv_one, panel_two, present_two, dinv_two):
    row = lax.axis_index("row")
    col = lax.axis_index("col")
    zl, x, core = row // 8, (row // 2) % 4, row % 2
    zh, y = col // 4, col % 4
    first = core == 0
    tie = lambda *values: lax.optimization_barrier(values)

    with jax.named_scope("spread"):
        take = lambda value: lax.dynamic_index_in_dim(value, 2 * zh + y // 2, 1, keepdims=False)
        own = to_plane(jnp.where(core == y % 2, take(panel_one), take(panel_two)))

    with jax.named_scope("swap"):
        other_blocks = to_core(ancestors)
        held_one, held_two, own = tie(panel_one, panel_two, own)
        mine = jnp.swapaxes(jnp.where(first, held_one, held_two), 2, 3)
        theirs = to_core(jnp.swapaxes(jnp.where(first, held_two, held_one), 2, 3))

    present = jnp.where(first, present_one, present_two)
    x_from = ((x + jnp.array([0, 3, 1, 2], jnp.int32)) % 4)[:, None]
    z_from = (zl ^ jnp.arange(4, dtype=jnp.int32))[None, :]
    spots = chunk_spot(z_from, x_from, zh, y)
    live_near = lax.dynamic_slice_in_dim(present, 4 * row, 4, 1)
    live_far = lax.dynamic_slice_in_dim(present, 4 * (row ^ 1), 4, 1)
    scal = jnp.concatenate(
        [
            spots.reshape(16),
            jnp.transpose(live_near).reshape(8),
            jnp.transpose(live_far).reshape(8),
            jnp.stack([y, zh]),
            jnp.transpose(lax.dynamic_slice_in_dim(present, 16 * col, 16, 1)).reshape(32),
        ]
    ).astype(jnp.int32)

    with jax.named_scope("gather"):
        parts = [own] + [to_zl(own, k) for k in (1, 2, 3)]
        a0, b0 = [jnp.stack([part[k] for part in parts]) for k in range(2)]
        a0, b0, other_blocks, theirs = tie(a0, b0, other_blocks, theirs)
        a1, b2 = along_x(a0, 1), along_x(b0, -1)
        b1, a2 = along_x(b0, 1), along_x(a0, -1)
        a3, b3 = along_x(a1, 1), along_x(b2, -1)
    with jax.named_scope("product"):
        acc = first_products(scal, ancestors, other_blocks, [a0, b0, a1, b1, a2, b2])
        out = second_products(scal, acc, ancestors, other_blocks, [a3, b3], mine, theirs)

    def shares(value, spot, move):
        at = lambda k: lax.dynamic_index_in_dim(value, spot ^ k, 0, keepdims=False)
        one, two, three = [move(at(k), k) for k in (1, 2, 3)]
        return (at(0) + one) + (two + three)

    def collect(value, spot, move):
        stack = jnp.stack([value] + [move(value, k) for k in (1, 2, 3)])
        return jnp.stack(
            [lax.dynamic_index_in_dim(stack, spot ^ k, 0, keepdims=False) for k in range(4)]
        )

    with jax.named_scope("diag"):
        piece = shares(out[4].reshape(4, 128, 256), y, to_y)
        piece = shares(piece.reshape(4, 32, 256), x, to_x)
        one, two, three = [to_zl(piece, k) for k in (1, 2, 3)]
        piece = (piece + one) + (two + three)
    with jax.named_scope("column"):
        got = [to_y(out[m], m) for m in (1, 2, 3)]
        piece, got[0] = tie(piece, got[0])
        piece = piece + to_zh(piece)
        keep, give = totals(out[0], got)
        got = to_zh(give)
        block = keep + decode(got[:, :256], got[:, 256:257])
    with jax.named_scope("back"):
        piece = tie(piece, keep)[0]
        part = collect(piece, x, to_x).reshape(128, 256)
        whole = collect(part, y, to_y).reshape(2, 256, 256)
        near, far = block[0], to_core(block[1])
        whole = tie(whole, far)[0]
        partner = to_core(whole)
    return (
        jnp.where(first, near, far)[None],
        dinv_one.astype(F32) - jnp.where(first, whole, partner),
        jnp.where(first, far, near)[None],
        dinv_two.astype(F32) - jnp.where(first, partner, whole),
    )


def solution(mesh):
    in_specs = (
        P("row", "col", None, None),
        P(None, "row", None, None),
        P(),
        P(),
        P(None, "row", None, None),
        P(),
        P(),
    )
    out_specs = (P(("row", "col"), None, None), P(), P(("row", "col"), None, None), P())
    return jax.shard_map(body, mesh=mesh, in_specs=in_specs, out_specs=out_specs, check_vma=False)
```

```python
import jax
import jax.numpy as jnp
from jax import lax
from jax.experimental import pallas as pl
from jax.experimental.pallas import tpu as pltpu
from jax.sharding import PartitionSpec as P

F32 = jnp.float32
BF16 = jnp.bfloat16
CODE = jnp.int16
AXES = ("row", "col")


def split_id(dev):
    row, col = dev // 8, dev % 8
    return row // 8, (row // 2) % 4, row % 2, col // 4, col % 4


def join_id(zl, x, core, zh, y):
    return ((zl * 4 + x) * 2 + core) * 8 + zh * 4 + y


def send(value, where):
    pairs = [(dev, join_id(*where(*split_id(dev)))) for dev in range(256)]
    return lax.ppermute(value, AXES, pairs)


def to_core(value):
    return send(value, lambda zl, x, core, zh, y: (zl, x, core ^ 1, zh, y))


def to_x(value, k):
    return send(value, lambda zl, x, core, zh, y: (zl, x ^ k, core, zh, y))


def along_x(value, k):
    return send(value, lambda zl, x, core, zh, y: (zl, (x + k) % 4, core, zh, y))


def to_zl(value, k):
    return send(value, lambda zl, x, core, zh, y: (zl ^ k, x, core, zh, y))


def to_y(value, k):
    return send(value, lambda zl, x, core, zh, y: (zl, x, core, zh, y ^ k))


def to_zh(value):
    return send(value, lambda zl, x, core, zh, y: (zl, x, core, zh ^ 1, y))


def plane_spot(zl, x, core, zh, y):
    h, bit = x % 2, y // 2
    x_to = (x + (2 * h - 1) * bit) % 4
    z_to = 2 * (zh ^ (zl // 2) ^ (zl % 2)) + (core ^ (zl // 2))
    return z_to, x_to, core ^ (y % 2), zl // 2, 2 * (zl % 2) + x // 2


def to_plane(value, flip):
    def where(*place):
        zl, *rest = plane_spot(*place)
        return zl ^ flip, *rest

    return send(value, where)


def chunk_spot(zl, x, zh, y):
    u = (x - 2 * (y % 2)) % 4
    h = jnp.where((u == 1) | (u == 2), 1, 0)
    bit = jnp.where(u >= 2, 1, 0)
    return 8 * h + 4 * ((zl % 2) ^ zh) + 2 * ((zl // 2) ^ zh ^ (y // 2)) + bit


def encode(value):
    peak = jnp.max(jnp.abs(value), axis=0, keepdims=True)
    power = jnp.floor(jnp.log2(jnp.maximum(peak, 1e-30))) + 1.0
    scaled = jnp.round(value * jnp.exp2(15.0 - power))
    code = jnp.clip(scaled, -32767.0, 32767.0).astype(jnp.int32).astype(CODE)
    mark = jnp.broadcast_to(power, (16, value.shape[1])).astype(jnp.int32).astype(CODE)
    return code, mark


def decode(code, mark):
    return code.astype(jnp.int32).astype(F32) * jnp.exp2(mark.astype(jnp.int32).astype(F32) - 15.0)


def first_kernel(scal, near, far, a0, b0, a1, b1, a2, b2, acc_ref, wide):
    step = pl.program_id(0)

    @pl.when(step == 0)
    def _():
        for k, group in enumerate(((a0, a1, a2), (b0, b1, b2))):
            for m, piece in enumerate(group):
                for z in range(4):
                    at = (4 * m + z) * 256
                    live = scal[34 + 2 * scal[4 * m + z] + k] > 0
                    value = jnp.where(live, piece[z], jnp.zeros((256, 256), BF16))
                    wide[at : at + 256, k * 256 : (k + 1) * 256] = value

    for side, blocks in enumerate((near, far)):
        acc = jnp.zeros((256, 512), F32)
        for pos in range(12):
            acc += jnp.dot(
                blocks[0, scal[pos]],
                wide[pos * 256 : (pos + 1) * 256, :],
                preferred_element_type=F32,
            )
        acc_ref[side, 0] = acc


def second_kernel(
    scal, acc_in, near, far, a3, b3, left_near, left_far, own, q1, q2, q3, diag_ref, wide
):
    step = pl.program_id(0)

    @pl.when(step == 0)
    def _():
        diag_ref[...] = jnp.zeros_like(diag_ref)
        for k, piece in enumerate((a3, b3)):
            for z in range(4):
                live = scal[34 + 2 * scal[12 + z] + k] > 0
                value = jnp.where(live, piece[z], jnp.zeros((256, 256), BF16))
                wide[z * 256 : (z + 1) * 256, k * 256 : (k + 1) * 256] = value

    zrel = (step // 2) ^ scal[33]
    for side, (blocks, left) in enumerate(((near, left_near), (far, left_far))):
        acc = acc_in[side, 0]
        for z in range(4):
            acc += jnp.dot(
                blocks[0, scal[12 + z] & 7],
                wide[z * 256 : (z + 1) * 256, :],
                preferred_element_type=F32,
            )
        for k in range(2):
            live = (-scal[16 + 8 * side + 2 * step + k]).astype(F32)
            term = acc[:, k * 256 : (k + 1) * 256] * live
            high = term.astype(BF16)
            rest = (term - high.astype(F32)).astype(BF16)
            both = jnp.concatenate([high, rest], axis=1)
            both = jnp.dot(left[k, 0], both, preferred_element_type=F32)
            diag_ref[k] += both[:, :256] + both[:, 256:]
            code, mark = encode(term)
            to = (2 * lax.rem(step, 2) + k) ^ scal[32]

            @pl.when(to == 0)
            def _():
                own[zrel, side] = term

            for m, ref in ((1, q1), (2, q2), (3, q3)):

                @pl.when(to == m)
                def _():
                    ref[zrel, side, 0:256] = code
                    ref[zrel, side, 256:272] = mark


def full(shape):
    return pl.BlockSpec(shape, lambda i, s: (0,) * len(shape))


PARAMS = pltpu.CompilerParams(dimension_semantics=("arbitrary",), vmem_limit_bytes=48 * 2**20)


def first_products(scal, near, far, pieces):
    return pl.pallas_call(
        first_kernel,
        grid_spec=pltpu.PrefetchScalarGridSpec(
            num_scalar_prefetch=1,
            grid=(4,),
            in_specs=[
                pl.BlockSpec((1, 16, 256, 256), lambda i, s: (i, 0, 0, 0)),
                pl.BlockSpec((1, 16, 256, 256), lambda i, s: (i, 0, 0, 0)),
            ]
            + [full(p.shape) for p in pieces],
            out_specs=pl.BlockSpec((2, 1, 256, 512), lambda i, s: (0, i, 0, 0)),
            scratch_shapes=[pltpu.VMEM((3072, 512), BF16)],
        ),
        out_shape=jax.ShapeDtypeStruct((2, 4, 256, 512), F32),
        cost_estimate=pl.CostEstimate(
            flops=2 * 2048 * 3072 * 512, transcendentals=0, bytes_accessed=24 * 2**20
        ),
        compiler_params=PARAMS,
    )(scal, near, far, *pieces)


def second_products(scal, acc, near, far, pieces, left_near, left_far):
    return pl.pallas_call(
        second_kernel,
        grid_spec=pltpu.PrefetchScalarGridSpec(
            num_scalar_prefetch=1,
            grid=(4,),
            in_specs=[
                pl.BlockSpec((2, 1, 256, 512), lambda i, s: (0, i, 0, 0)),
                pl.BlockSpec((1, 8, 256, 256), lambda i, s: (i, s[12] // 8, 0, 0)),
                pl.BlockSpec((1, 8, 256, 256), lambda i, s: (i, s[12] // 8, 0, 0)),
            ]
            + [full(p.shape) for p in pieces]
            + [
                pl.BlockSpec((2, 1, 256, 256), lambda i, s: (0, i, 0, 0)),
                pl.BlockSpec((2, 1, 256, 256), lambda i, s: (0, i, 0, 0)),
            ],
            out_specs=[
                full((2, 2, 256, 256)),
                full((2, 2, 272, 256)),
                full((2, 2, 272, 256)),
                full((2, 2, 272, 256)),
                full((2, 256, 256)),
            ],
            scratch_shapes=[pltpu.VMEM((1024, 512), BF16)],
        ),
        out_shape=[jax.ShapeDtypeStruct((2, 2, 256, 256), F32)]
        + [jax.ShapeDtypeStruct((2, 2, 272, 256), CODE)] * 3
        + [jax.ShapeDtypeStruct((2, 256, 256), F32)],
        cost_estimate=pl.CostEstimate(
            flops=2 * 2048 * 1024 * 512, transcendentals=0, bytes_accessed=16 * 2**20
        ),
        compiler_params=PARAMS,
    )(scal, acc, near, far, *pieces, left_near, left_far)


def total_kernel(own, q1, q2, q3, keep, give):
    for z in range(2):
        for side in range(2):
            value = own[z, side]
            for ref in (q1, q2, q3):
                value += decode(ref[z, side, 0:256], ref[z, side, 256:257])
            if z == 0:
                keep[side] = value
            else:
                code, mark = encode(value)
                give[side, 0:256] = code
                give[side, 256:272] = mark


def totals(own, others):
    return pl.pallas_call(
        total_kernel,
        out_shape=[
            jax.ShapeDtypeStruct((2, 256, 256), F32),
            jax.ShapeDtypeStruct((2, 272, 256), CODE),
        ],
        compiler_params=pltpu.CompilerParams(vmem_limit_bytes=32 * 2**20),
    )(own, *others)


def products(scal, near, far, pieces, left_near, left_far):
    early = lambda i: jnp.minimum(i, 3)
    late = lambda i: jnp.maximum(i - 4, 0)
    full = lambda shape: pl.BlockSpec(shape, lambda i, s: (0,) * len(shape))
    return pl.pallas_call(
        product_kernel,
        grid_spec=pltpu.PrefetchScalarGridSpec(
            num_scalar_prefetch=1,
            grid=(4,),
            in_specs=[
                pl.BlockSpec((1, 16, 256, 256), lambda i, s: (i, 0, 0, 0)),
                pl.BlockSpec((1, 16, 256, 256), lambda i, s: (i, 0, 0, 0)),
            ]
            + [full(p.shape) for p in pieces]
            + [
                pl.BlockSpec((2, 1, 256, 256), lambda i, s: (0, i, 0, 0)),
                pl.BlockSpec((2, 1, 256, 256), lambda i, s: (0, i, 0, 0)),
            ],
            out_specs=[
                full((2, 2, 256, 256)),
                full((2, 2, 272, 256)),
                full((2, 2, 272, 256)),
                full((2, 2, 272, 256)),
                full((2, 256, 256)),
            ],
            scratch_shapes=[pltpu.VMEM((4096, 2 * 256), BF16)],
        ),
        out_shape=[jax.ShapeDtypeStruct((2, 2, 256, 256), F32)]
        + [jax.ShapeDtypeStruct((2, 2, 272, 256), CODE)] * 3
        + [jax.ShapeDtypeStruct((2, 256, 256), F32)],
        cost_estimate=pl.CostEstimate(
            flops=2 * 2048 * 4096 * 2 * 256, transcendentals=0, bytes_accessed=24 * 2**20
        ),
        compiler_params=pltpu.CompilerParams(
            dimension_semantics=("arbitrary",), vmem_limit_bytes=48 * 2**20
        ),
    )(scal, near, far, *pieces, left_near, left_far)


def body(ancestors, panel_one, present_one, dinv_one, panel_two, present_two, dinv_two):
    row = lax.axis_index("row")
    col = lax.axis_index("col")
    zl, x, core = row // 8, (row // 2) % 4, row % 2
    zh, y = col // 4, col % 4
    first = core == 0
    tie = lambda *values: lax.optimization_barrier(values)

    with jax.named_scope("spread"):
        take = lambda value: lax.dynamic_index_in_dim(value, 2 * zh + y // 2, 1, keepdims=False)
        own = jnp.where(core == y % 2, take(panel_one), take(panel_two))
        own = [to_plane(own, 0), to_plane(own, 2)]

    with jax.named_scope("swap"):
        other_blocks = to_core(ancestors)
        mine = jnp.swapaxes(jnp.where(first, panel_one, panel_two), 2, 3)
        theirs = to_core(jnp.swapaxes(jnp.where(first, panel_two, panel_one), 2, 3))

    present = jnp.where(first, present_one, present_two)
    x_from = ((x + jnp.array([0, 3, 1, 2], jnp.int32)) % 4)[:, None]
    z_from = (zl ^ jnp.array([0, 2, 1, 2 ^ 1], jnp.int32))[None, :]
    spots = chunk_spot(z_from, x_from, zh, y)
    live_near = lax.dynamic_slice_in_dim(present, 4 * row, 4, 1)
    live_far = lax.dynamic_slice_in_dim(present, 4 * (row ^ 1), 4, 1)
    scal = jnp.concatenate(
        [
            spots.reshape(16),
            jnp.transpose(live_near).reshape(8),
            jnp.transpose(live_far).reshape(8),
            jnp.stack([y, zh]),
            jnp.transpose(lax.dynamic_slice_in_dim(present, 16 * col, 16, 1)).reshape(32),
        ]
    ).astype(jnp.int32)

    with jax.named_scope("gather"):
        parts = own + [to_zl(part, 1) for part in own]
        a0, b0 = [jnp.stack([part[k] for part in parts]) for k in range(2)]
        a0, b0, other_blocks, theirs = tie(a0, b0, other_blocks, theirs)
        a1, b2 = along_x(a0, 1), along_x(b0, -1)
        b1, a2 = along_x(b0, 1), along_x(a0, -1)
        a3, b3 = along_x(a1, 1), along_x(b2, -1)
    with jax.named_scope("product"):
        acc = first_products(scal, ancestors, other_blocks, [a0, b0, a1, b1, a2, b2])
        out = second_products(scal, acc, ancestors, other_blocks, [a3, b3], mine, theirs)

    def shares(value, spot, move):
        at = lambda k: lax.dynamic_index_in_dim(value, spot ^ k, 0, keepdims=False)
        one, two, three = [move(at(k), k) for k in (1, 2, 3)]
        return (at(0) + one) + (two + three)

    def collect(value, spot, move):
        stack = jnp.stack([value] + [move(value, k) for k in (1, 2, 3)])
        return jnp.stack(
            [lax.dynamic_index_in_dim(stack, spot ^ k, 0, keepdims=False) for k in range(4)]
        )

    with jax.named_scope("diag"):
        piece = shares(out[4].reshape(4, 128, 256), y, to_y)
        piece = shares(piece.reshape(4, 32, 256), x, to_x)
        one, two, three = [to_zl(piece, k) for k in (1, 2, 3)]
        piece = (piece + one) + (two + three)
    with jax.named_scope("column"):
        got = [to_y(out[m], m) for m in (1, 2, 3)]
        piece, got[0] = tie(piece, got[0])
        piece = piece + to_zh(piece)
        keep, give = totals(out[0], got)
        got = to_zh(give)
        block = keep + decode(got[:, :256], got[:, 256:257])
    with jax.named_scope("back"):
        piece = tie(piece, keep)[0]
        part = collect(piece, x, to_x).reshape(128, 256)
        whole = collect(part, y, to_y).reshape(2, 256, 256)
        near, far = block[0], to_core(block[1])
        whole = tie(whole, far)[0]
        partner = to_core(whole)
    return (
        jnp.where(first, near, far)[None],
        dinv_one.astype(F32) - jnp.where(first, whole, partner),
        jnp.where(first, far, near)[None],
        dinv_two.astype(F32) - jnp.where(first, partner, whole),
    )


def solution(mesh):
    in_specs = (
        P("row", "col", None, None),
        P(None, "row", None, None),
        P(),
        P(),
        P(None, "row", None, None),
        P(),
        P(),
    )
    out_specs = (P(("row", "col"), None, None), P(), P(("row", "col"), None, None), P())
    return jax.shard_map(body, mesh=mesh, in_specs=in_specs, out_specs=out_specs, check_vma=False)
```

```python
import jax
import jax.numpy as jnp
from jax import lax
from jax.experimental import pallas as pl
from jax.experimental.pallas import tpu as pltpu
from jax.sharding import PartitionSpec as P

F32 = jnp.float32
BF16 = jnp.bfloat16
CODE = jnp.int16
AXES = ("row", "col")


def split_id(dev):
    row, col = dev // 8, dev % 8
    return row // 8, (row // 2) % 4, row % 2, col // 4, col % 4


def join_id(zl, x, core, zh, y):
    return ((zl * 4 + x) * 2 + core) * 8 + zh * 4 + y


def send(value, where):
    pairs = [(dev, join_id(*where(*split_id(dev)))) for dev in range(256)]
    return lax.ppermute(value, AXES, pairs)


def to_core(value):
    return send(value, lambda zl, x, core, zh, y: (zl, x, core ^ 1, zh, y))


def to_x(value, k):
    return send(value, lambda zl, x, core, zh, y: (zl, x ^ k, core, zh, y))


def along_x(value, k):
    return send(value, lambda zl, x, core, zh, y: (zl, (x + k) % 4, core, zh, y))


def to_zl(value, k):
    return send(value, lambda zl, x, core, zh, y: (zl ^ k, x, core, zh, y))


def to_y(value, k):
    return send(value, lambda zl, x, core, zh, y: (zl, x, core, zh, y ^ k))


def to_zh(value):
    return send(value, lambda zl, x, core, zh, y: (zl, x, core, zh ^ 1, y))


def plane_spot(zl, x, core, zh, y):
    h, bit = x % 2, y // 2
    x_to = (x + (2 * h - 1) * bit) % 4
    z_to = 2 * (zh ^ (zl // 2) ^ (zl % 2)) + (core ^ (zl // 2))
    return z_to, x_to, core ^ (y % 2), zl // 2, 2 * (zl % 2) + x // 2


def to_plane(value, flip):
    def where(*place):
        zl, *rest = plane_spot(*place)
        return zl ^ flip, *rest

    return send(value, where)


def chunk_spot(zl, x, zh, y):
    u = (x - 2 * (y % 2)) % 4
    h = jnp.where((u == 1) | (u == 2), 1, 0)
    bit = jnp.where(u >= 2, 1, 0)
    return 8 * h + 4 * ((zl % 2) ^ zh) + 2 * ((zl // 2) ^ zh ^ (y // 2)) + bit


def encode(value):
    peak = jnp.max(jnp.abs(value), axis=0, keepdims=True)
    power = jnp.floor(jnp.log2(jnp.maximum(peak, 1e-30))) + 1.0
    scaled = jnp.round(value * jnp.exp2(15.0 - power))
    code = jnp.clip(scaled, -32767.0, 32767.0).astype(jnp.int32).astype(CODE)
    mark = jnp.broadcast_to(power, (16, value.shape[1])).astype(jnp.int32).astype(CODE)
    return code, mark


def decode(code, mark):
    return code.astype(jnp.int32).astype(F32) * jnp.exp2(mark.astype(jnp.int32).astype(F32) - 15.0)


def first_kernel(scal, near, far, a0, b0, a1, b1, a2, b2, acc_ref, wide):
    step = pl.program_id(0)

    @pl.when(step == 0)
    def _():
        for k, group in enumerate(((a0, a1, a2), (b0, b1, b2))):
            for m, piece in enumerate(group):
                for z in range(4):
                    at = (4 * m + z) * 256
                    live = scal[34 + 2 * scal[4 * m + z] + k] > 0
                    value = jnp.where(live, piece[z], jnp.zeros((256, 256), BF16))
                    wide[at : at + 256, k * 256 : (k + 1) * 256] = value

    for side, blocks in enumerate((near, far)):
        acc = jnp.zeros((256, 512), F32)
        for pos in range(12):
            acc += jnp.dot(
                blocks[0, scal[pos]],
                wide[pos * 256 : (pos + 1) * 256, :],
                preferred_element_type=F32,
            )
        acc_ref[side, 0] = acc


def second_kernel(
    scal, acc_in, near, far, a3, b3, left_near, left_far, own, q1, q2, q3, diag_ref, wide
):
    step = pl.program_id(0)

    @pl.when(step == 0)
    def _():
        diag_ref[...] = jnp.zeros_like(diag_ref)
        for k, piece in enumerate((a3, b3)):
            for z in range(4):
                live = scal[34 + 2 * scal[12 + z] + k] > 0
                value = jnp.where(live, piece[z], jnp.zeros((256, 256), BF16))
                wide[z * 256 : (z + 1) * 256, k * 256 : (k + 1) * 256] = value

    zrel = (step // 2) ^ scal[33]
    for side, (blocks, left) in enumerate(((near, left_near), (far, left_far))):
        acc = acc_in[side, 0]
        for z in range(4):
            acc += jnp.dot(
                blocks[0, scal[12 + z] & 7],
                wide[z * 256 : (z + 1) * 256, :],
                preferred_element_type=F32,
            )
        for k in range(2):
            live = (-scal[16 + 8 * side + 2 * step + k]).astype(F32)
            term = acc[:, k * 256 : (k + 1) * 256] * live
            high = term.astype(BF16)
            rest = (term - high.astype(F32)).astype(BF16)
            both = jnp.concatenate([high, rest], axis=1)
            both = jnp.dot(left[k, 0], both, preferred_element_type=F32)
            diag_ref[k] += both[:, :256] + both[:, 256:]
            code, mark = encode(term)
            to = (2 * lax.rem(step, 2) + k) ^ scal[32]

            @pl.when(to == 0)
            def _():
                own[zrel, side] = term

            for m, ref in ((1, q1), (2, q2), (3, q3)):

                @pl.when(to == m)
                def _():
                    ref[zrel, side, 0:256] = code
                    ref[zrel, side, 256:272] = mark


def full(shape):
    return pl.BlockSpec(shape, lambda i, s: (0,) * len(shape))


PARAMS = pltpu.CompilerParams(dimension_semantics=("arbitrary",), vmem_limit_bytes=48 * 2**20)


def first_products(scal, near, far, pieces):
    return pl.pallas_call(
        first_kernel,
        grid_spec=pltpu.PrefetchScalarGridSpec(
            num_scalar_prefetch=1,
            grid=(4,),
            in_specs=[
                pl.BlockSpec((1, 16, 256, 256), lambda i, s: (i, 0, 0, 0)),
                pl.BlockSpec((1, 16, 256, 256), lambda i, s: (i, 0, 0, 0)),
            ]
            + [full(p.shape) for p in pieces],
            out_specs=pl.BlockSpec((2, 1, 256, 512), lambda i, s: (0, i, 0, 0)),
            scratch_shapes=[pltpu.VMEM((3072, 512), BF16)],
        ),
        out_shape=jax.ShapeDtypeStruct((2, 4, 256, 512), F32),
        cost_estimate=pl.CostEstimate(
            flops=2 * 2048 * 3072 * 512, transcendentals=0, bytes_accessed=24 * 2**20
        ),
        compiler_params=PARAMS,
    )(scal, near, far, *pieces)


def second_products(scal, acc, near, far, pieces, left_near, left_far):
    return pl.pallas_call(
        second_kernel,
        grid_spec=pltpu.PrefetchScalarGridSpec(
            num_scalar_prefetch=1,
            grid=(4,),
            in_specs=[
                pl.BlockSpec((2, 1, 256, 512), lambda i, s: (0, i, 0, 0)),
                pl.BlockSpec((1, 8, 256, 256), lambda i, s: (i, s[12] // 8, 0, 0)),
                pl.BlockSpec((1, 8, 256, 256), lambda i, s: (i, s[12] // 8, 0, 0)),
            ]
            + [full(p.shape) for p in pieces]
            + [
                pl.BlockSpec((2, 1, 256, 256), lambda i, s: (0, i, 0, 0)),
                pl.BlockSpec((2, 1, 256, 256), lambda i, s: (0, i, 0, 0)),
            ],
            out_specs=[
                full((2, 2, 256, 256)),
                full((2, 2, 272, 256)),
                full((2, 2, 272, 256)),
                full((2, 2, 272, 256)),
                full((2, 256, 256)),
            ],
            scratch_shapes=[pltpu.VMEM((1024, 512), BF16)],
        ),
        out_shape=[jax.ShapeDtypeStruct((2, 2, 256, 256), F32)]
        + [jax.ShapeDtypeStruct((2, 2, 272, 256), CODE)] * 3
        + [jax.ShapeDtypeStruct((2, 256, 256), F32)],
        cost_estimate=pl.CostEstimate(
            flops=2 * 2048 * 1024 * 512, transcendentals=0, bytes_accessed=16 * 2**20
        ),
        compiler_params=PARAMS,
    )(scal, acc, near, far, *pieces, left_near, left_far)


def total_kernel(own, q1, q2, q3, keep, give):
    for z in range(2):
        for side in range(2):
            value = own[z, side]
            for ref in (q1, q2, q3):
                value += decode(ref[z, side, 0:256], ref[z, side, 256:257])
            if z == 0:
                keep[side] = value
            else:
                code, mark = encode(value)
                give[side, 0:256] = code
                give[side, 256:272] = mark


def totals(own, others):
    return pl.pallas_call(
        total_kernel,
        out_shape=[
            jax.ShapeDtypeStruct((2, 256, 256), F32),
            jax.ShapeDtypeStruct((2, 272, 256), CODE),
        ],
        compiler_params=pltpu.CompilerParams(vmem_limit_bytes=32 * 2**20),
    )(own, *others)


def products(scal, near, far, pieces, left_near, left_far):
    early = lambda i: jnp.minimum(i, 3)
    late = lambda i: jnp.maximum(i - 4, 0)
    full = lambda shape: pl.BlockSpec(shape, lambda i, s: (0,) * len(shape))
    return pl.pallas_call(
        product_kernel,
        grid_spec=pltpu.PrefetchScalarGridSpec(
            num_scalar_prefetch=1,
            grid=(4,),
            in_specs=[
                pl.BlockSpec((1, 16, 256, 256), lambda i, s: (i, 0, 0, 0)),
                pl.BlockSpec((1, 16, 256, 256), lambda i, s: (i, 0, 0, 0)),
            ]
            + [full(p.shape) for p in pieces]
            + [
                pl.BlockSpec((2, 1, 256, 256), lambda i, s: (0, i, 0, 0)),
                pl.BlockSpec((2, 1, 256, 256), lambda i, s: (0, i, 0, 0)),
            ],
            out_specs=[
                full((2, 2, 256, 256)),
                full((2, 2, 272, 256)),
                full((2, 2, 272, 256)),
                full((2, 2, 272, 256)),
                full((2, 256, 256)),
            ],
            scratch_shapes=[pltpu.VMEM((4096, 2 * 256), BF16)],
        ),
        out_shape=[jax.ShapeDtypeStruct((2, 2, 256, 256), F32)]
        + [jax.ShapeDtypeStruct((2, 2, 272, 256), CODE)] * 3
        + [jax.ShapeDtypeStruct((2, 256, 256), F32)],
        cost_estimate=pl.CostEstimate(
            flops=2 * 2048 * 4096 * 2 * 256, transcendentals=0, bytes_accessed=24 * 2**20
        ),
        compiler_params=pltpu.CompilerParams(
            dimension_semantics=("arbitrary",), vmem_limit_bytes=48 * 2**20
        ),
    )(scal, near, far, *pieces, left_near, left_far)


def body(ancestors, panel_one, present_one, dinv_one, panel_two, present_two, dinv_two):
    row = lax.axis_index("row")
    col = lax.axis_index("col")
    zl, x, core = row // 8, (row // 2) % 4, row % 2
    zh, y = col // 4, col % 4
    first = core == 0
    tie = lambda *values: lax.optimization_barrier(values)

    with jax.named_scope("spread"):
        take = lambda value: lax.dynamic_index_in_dim(value, 2 * zh + y // 2, 1, keepdims=False)
        own = jnp.where(core == y % 2, take(panel_one), take(panel_two))
        own = [to_plane(own, 0), to_plane(own, 2)]

    with jax.named_scope("swap"):
        other_blocks = to_core(ancestors)
        mine = jnp.swapaxes(jnp.where(first, panel_one, panel_two), 2, 3)
        theirs = to_core(jnp.swapaxes(jnp.where(first, panel_two, panel_one), 2, 3))

    present = jnp.where(first, present_one, present_two)
    x_from = ((x + jnp.array([0, 3, 1, 2], jnp.int32)) % 4)[:, None]
    z_from = (zl ^ jnp.array([0, 2, 1, 2 ^ 1], jnp.int32))[None, :]
    spots = chunk_spot(z_from, x_from, zh, y)
    live_near = lax.dynamic_slice_in_dim(present, 4 * row, 4, 1)
    live_far = lax.dynamic_slice_in_dim(present, 4 * (row ^ 1), 4, 1)
    scal = jnp.concatenate(
        [
            spots.reshape(16),
            jnp.transpose(live_near).reshape(8),
            jnp.transpose(live_far).reshape(8),
            jnp.stack([y, zh]),
            jnp.transpose(lax.dynamic_slice_in_dim(present, 16 * col, 16, 1)).reshape(32),
        ]
    ).astype(jnp.int32)

    with jax.named_scope("gather"):
        parts = own + [to_zl(part, 1) for part in own]
        a0, b0 = [jnp.stack([part[k] for part in parts]) for k in range(2)]
        a0, b0, other_blocks, theirs = tie(a0, b0, other_blocks, theirs)
        a1, b2 = along_x(a0, 1), along_x(b0, -1)
        b1, a2 = along_x(b0, 1), along_x(a0, -1)
        a3, b3 = along_x(a1, 1), along_x(b2, -1)
    with jax.named_scope("product"):
        acc = first_products(scal, ancestors, other_blocks, [a0, b0, a1, b1, a2, b2])
        out = second_products(scal, acc, ancestors, other_blocks, [a3, b3], mine, theirs)

    def shares(value, spot, move):
        at = lambda k: lax.dynamic_index_in_dim(value, spot ^ k, 0, keepdims=False)
        one, two, three = [move(at(k), k) for k in (1, 2, 3)]
        return (at(0) + one) + (two + three)

    def collect(value, spot, move):
        stack = jnp.stack([value] + [move(value, k) for k in (1, 2, 3)])
        return jnp.stack(
            [lax.dynamic_index_in_dim(stack, spot ^ k, 0, keepdims=False) for k in range(4)]
        )

    with jax.named_scope("diag"):
        piece = shares(out[4].reshape(4, 128, 256), y, to_y)
        piece = shares(piece.reshape(4, 32, 256), x, to_x)
        one, two, three = [to_zl(piece, k) for k in (1, 2, 3)]
        piece = (piece + one) + (two + three)
    with jax.named_scope("column"):
        got = [to_y(out[m], m) for m in (1, 2, 3)]
        piece, got[0] = tie(piece, got[0])
        piece = piece + to_zh(piece)
        keep, give = totals(out[0], got)
        got = to_zh(give)
        block = keep + decode(got[:, :256], got[:, 256:257])
    with jax.named_scope("back"):
        part = collect(piece, x, to_x).reshape(128, 256)
        part = tie(part, keep)[0]
        whole = collect(part, y, to_y).reshape(2, 256, 256)
        near, far = block[0], to_core(block[1])
        whole = tie(whole, far)[0]
        partner = to_core(whole)
    return (
        jnp.where(first, near, far)[None],
        dinv_one.astype(F32) - jnp.where(first, whole, partner),
        jnp.where(first, far, near)[None],
        dinv_two.astype(F32) - jnp.where(first, partner, whole),
    )


def solution(mesh):
    in_specs = (
        P("row", "col", None, None),
        P(None, "row", None, None),
        P(),
        P(),
        P(None, "row", None, None),
        P(),
        P(),
    )
    out_specs = (P(("row", "col"), None, None), P(), P(("row", "col"), None, None), P())
    return jax.shard_map(body, mesh=mesh, in_specs=in_specs, out_specs=out_specs, check_vma=False)
```
